32 devices in a mesh: group: 4 (over z), replica: 8 (over y, x, core).
Axes of the slice: x: 2, y: 2, z: 4, core: 2. Of those that a mesh axis runs over, the one named last changes fastest.
Arguments:
- inputs: bfloat16 [8, 512, 1024], P('replica', 'group'), may hold values from -6 to 6
- cotangent: bfloat16 [8, 512, 1024], P('replica', 'group'), may hold values from -6 to 6
- norm_gain: bfloat16 [2, 2, 1024], P(None, None, 'group'), may hold values from 0.5 to 1.5
- norm_bias: bfloat16 [2, 2, 1024], P(None, None, 'group'), may hold values from -4 to 4
- w_qkv: bfloat16 [2, 1024, 3072], P(None, 'group'), may hold values from -0.1875 to 0.1875
- bias_qv: bfloat16 [2, 2048], P(None, 'group'), may hold values from -6 to 6
- w_out: bfloat16 [2, 1024, 1024], P(None, 'group'), may hold values from -0.75 to 0.75
- bias_out: bfloat16 [2, 1024], P(None, 'group'), may hold values from -6 to 6
- w_up: bfloat16 [2, 1024, 4096], P(None, 'group'), may hold values from -0.1875 to 0.1875
- bias_up: bfloat16 [2, 4096], P(None, 'group'), may hold values from -6 to 6
- w_down: bfloat16 [2, 4096, 1024], P(None, 'group'), may hold values from -0.09375 to 0.09375
- bias_down: bfloat16 [2, 1024], P(None, 'group'), may hold values from -6 to 6
Outputs:
- outputs: bfloat16 [8, 512, 1024], P('replica', 'group')
- input_grad: float32 [8, 512, 1024], P('replica', 'group')
- grad_norm_gain: float32 [2, 2, 1024], P(None, None, 'group')
- grad_norm_bias: float32 [2, 2, 1024], P(None, None, 'group')
- grad_qkv: float32 [2, 1024, 3072], P(None, 'group')
- grad_qv_bias: float32 [2, 2048], P(None, 'group')
- grad_out: float32 [2, 1024, 1024], P(None, 'group')
- grad_out_bias: float32 [2, 1024], P(None, 'group')
- grad_up: float32 [2, 1024, 4096], P(None, 'group')
- grad_up_bias: float32 [2, 4096], P(None, 'group')
- grad_down: float32 [2, 4096, 1024], P(None, 'group')
- grad_down_bias: float32 [2, 1024], P(None, 'group')
The draws below stay inside these ranges and needn't reach their ends.
All inputs are finite; a program needn't handle non-finite values.
Results may differ from the reference program's by a relative error of at most 0.024.
Values may be sent and summed in bfloat16 or wider, within the bound.
A program may use at most 256 MiB of HBM per device.

```python
import jax
import jax.numpy as jnp
from jax import lax

D = 1024
HEADS = 16
HEAD_DIM = 64
FF = 4096
LAYERS = 2
SEQ_LEN = 512
SEQS = 8


def level_of(own_key, extent, pieces, low, high):
    factor_of = 1.0
    for position, shards_of in pieces:
        heights = jax.random.uniform(jax.random.fold_in(jax.random.fold_in(own_key, 6), position), (shards_of,), jnp.float32, low / len(pieces), high / len(pieces))
        factor_of = factor_of * jnp.repeat(jnp.exp(heights), extent[position] // shards_of).reshape((-1,) + (1,) * (len(extent) - 1 - position))
    return factor_of


def noise(key, shape, spread, most, shards=(), kind=jnp.bfloat16):
    factor_of = level_of(key, shape, shards, -0.22, 0.18) if shards else 1.0
    array = jax.random.normal(key, shape, jnp.float32) * spread * factor_of
    return jnp.minimum(jnp.maximum(array, -most), most).astype(kind)


def setup_inputs(seed: int = 0) -> dict:
    splits = jax.random.split(jax.random.key(seed), 13)
    return {
        "inputs": noise(splits[0], (SEQS, SEQ_LEN, D), 1.0, 6.0, ((0, 8), (1, 4))),
        "cotangent": noise(splits[1], (SEQS, SEQ_LEN, D), 1.0, 6.0, ((0, 8), (1, 4))),
        "norm_gain": jnp.clip(1.0 + 0.1 * jax.random.normal(splits[2], (LAYERS, 2, D), jnp.float32), 0.5, 1.5).astype(jnp.bfloat16),
        "norm_bias": noise(splits[3], (LAYERS, 2, D), 0.3, 4.0, ((2, 4),)),
        "w_qkv": noise(splits[4], (LAYERS, D, 3 * D), D ** -0.5, 0.1875, ((1, 4),)),
        "bias_qv": noise(splits[5], (LAYERS, 2 * D), 0.5, 6.0, ((1, 4),)),
        "w_out": noise(splits[6], (LAYERS, D, D), (D // 16) ** -0.5, 0.75, ((1, 4),)),
        "bias_out": noise(splits[7], (LAYERS, D), 0.5, 6.0, ((1, 4),)),
        "w_up": noise(splits[8], (LAYERS, D, FF), D ** -0.5, 0.1875, ((1, 4),)),
        "bias_up": noise(splits[9], (LAYERS, FF), 0.5, 6.0, ((1, 4),)),
        "w_down": noise(splits[10], (LAYERS, FF, D), FF ** -0.5, 0.09375, ((1, 4),)),
        "bias_down": noise(splits[11], (LAYERS, D), 0.5, 6.0, ((1, 4),)),
    }


EPS = 1e-05
NEG = -1e+30
GELU_C = 0.7978845608028654
GELU_A = 0.044715

def head_slopes():
    return 2.0 ** (-8.0 * (jnp.arange(HEADS, dtype=jnp.float32) + 1.0) / HEADS)

def norm_apply(values_in, gain_row, bias_row):
    row_mean = lax.optimization_barrier(jnp.mean(values_in, axis=-1, keepdims=True))
    centered = values_in - row_mean
    variance = lax.optimization_barrier(jnp.mean(centered * centered, axis=-1, keepdims=True))
    inverse = lax.rsqrt(variance + EPS)
    normed = centered * inverse
    return (normed * gain_row + bias_row, normed, inverse)

def norm_back(grad_in, normed, inverse, gain_row):
    scaled = grad_in * gain_row
    return inverse * (scaled - lax.optimization_barrier(jnp.mean(scaled, axis=-1, keepdims=True)) - normed * lax.optimization_barrier(jnp.mean(scaled * normed, axis=-1, keepdims=True)))

def gelu_parts(pre_act):
    tanh_val = jnp.tanh(GELU_C * (pre_act + GELU_A * pre_act * pre_act * pre_act))
    gelu_value = 0.5 * pre_act * (1.0 + tanh_val)
    gelu_slope = 0.5 * (1.0 + tanh_val) + 0.5 * pre_act * (1.0 - tanh_val * tanh_val) * GELU_C * (1.0 + 3.0 * GELU_A * pre_act * pre_act)
    return (gelu_value, gelu_slope)

def split_heads(matrix):
    return matrix.reshape(matrix.shape[0], HEADS, HEAD_DIM)

def attention_scores(queries, keys_all, q_pos, k_pos):
    raw_dots = jnp.einsum('qhd,khd->hqk', queries.astype(jnp.float32), keys_all.astype(jnp.float32))
    offset = (q_pos[:, None] - k_pos[None, :]).astype(jnp.float32)
    scores = raw_dots * HEAD_DIM ** (-0.5) - head_slopes()[:, None, None] * offset[None, :, :]
    return jnp.where((offset >= 0.0)[None, :, :], scores, NEG)

def attend(queries, keys_all, values_all, q_pos, k_pos):
    scores = attention_scores(queries, keys_all, q_pos, k_pos)
    row_top = lax.optimization_barrier(jnp.max(scores, axis=-1, keepdims=True))
    exps_raw = jnp.exp(scores - row_top)
    row_total = lax.optimization_barrier(jnp.sum(exps_raw, axis=-1, keepdims=True))
    log_total = row_top + jnp.log(row_total)
    probs_b16 = jnp.exp(scores - log_total).astype(jnp.bfloat16)
    context = jnp.einsum('hqk,khd->qhd', probs_b16.astype(jnp.float32), values_all.astype(jnp.float32))
    return (context.astype(jnp.bfloat16), log_total)

def attend_back(d_context, context, queries, keys_all, values_all, log_total, q_pos, k_pos):
    scores = attention_scores(queries, keys_all, q_pos, k_pos)
    probs = jnp.exp(scores - log_total)
    probs_b16 = probs.astype(jnp.bfloat16)
    d_probs = jnp.einsum('qhd,khd->hqk', d_context.astype(jnp.float32), values_all.astype(jnp.float32))
    row_delta = lax.optimization_barrier(jnp.sum(d_context.astype(jnp.float32) * context.astype(jnp.float32), axis=-1))
    d_scores = (probs * (d_probs - row_delta.T[:, :, None])).astype(jnp.bfloat16)
    d_query = jnp.einsum('hqk,khd->qhd', d_scores.astype(jnp.float32), keys_all.astype(jnp.float32)) * HEAD_DIM ** (-0.5)
    d_keys = jnp.einsum('hqk,qhd->khd', d_scores.astype(jnp.float32), queries.astype(jnp.float32)) * HEAD_DIM ** (-0.5)
    d_values = jnp.einsum('hqk,qhd->khd', probs_b16.astype(jnp.float32), d_context.astype(jnp.float32))
    return (d_query, d_keys, d_values)

def forward_layer(activation, layer_params, positions):
    norm_g, norm_b, w_qkv, bias_qv, w_out, bias_out, w_up, bias_up, w_down, bias_down = layer_params
    model_width = activation.shape[1]
    normed_in, normed_a, inverse_a = norm_apply(activation, norm_g[0].astype(jnp.float32), norm_b[0].astype(jnp.float32))
    attn_in = normed_in.astype(jnp.bfloat16)
    projected = jnp.dot(attn_in, w_qkv, preferred_element_type=jnp.float32)
    bias_f = bias_qv.astype(jnp.float32)
    queries = split_heads((projected[:, :model_width] + bias_f[:model_width]).astype(jnp.bfloat16))
    keys_all = split_heads(projected[:, model_width:2 * model_width].astype(jnp.bfloat16))
    values_all = split_heads((projected[:, 2 * model_width:] + bias_f[model_width:]).astype(jnp.bfloat16))
    context, log_total = attend(queries, keys_all, values_all, positions, positions)
    context = context.reshape(-1, model_width)
    middle = activation + jnp.dot(context, w_out, preferred_element_type=jnp.float32) + bias_out.astype(jnp.float32)
    mlp_norm, normed_b, inverse_b = norm_apply(middle, norm_g[1].astype(jnp.float32), norm_b[1].astype(jnp.float32))
    mlp_in = mlp_norm.astype(jnp.bfloat16)
    pre_act = jnp.dot(mlp_in, w_up, preferred_element_type=jnp.float32) + bias_up.astype(jnp.float32)
    gelu_value, gelu_slope = gelu_parts(pre_act)
    hidden = gelu_value.astype(jnp.bfloat16)
    result = middle + jnp.dot(hidden, w_down, preferred_element_type=jnp.float32) + bias_down.astype(jnp.float32)
    saved_acts = (normed_a, inverse_a, attn_in, queries, keys_all, values_all, log_total, context, normed_b, inverse_b, mlp_in, gelu_slope, hidden)
    return (result, saved_acts)

def backward_layer(grad_out, layer_params, saved_acts, positions):
    norm_g, norm_b, w_qkv, bias_qv, w_out, bias_out, w_up, bias_up, w_down, bias_down = layer_params
    normed_a, inverse_a, attn_in, queries, keys_all, values_all, log_total, context, normed_b, inverse_b, mlp_in, gelu_slope, hidden = saved_acts
    model_width = grad_out.shape[1]
    grad_b16 = grad_out.astype(jnp.bfloat16)
    g_down = jnp.dot(hidden.T, grad_b16, preferred_element_type=jnp.float32)
    g_down_bias = lax.optimization_barrier(jnp.sum(grad_out, axis=0))
    d_hidden = jnp.dot(grad_b16, w_down.T, preferred_element_type=jnp.float32)
    d_pre = d_hidden * gelu_slope
    g_up_bias = lax.optimization_barrier(jnp.sum(d_pre, axis=0))
    pre_b16 = d_pre.astype(jnp.bfloat16)
    g_up = jnp.dot(mlp_in.T, pre_b16, preferred_element_type=jnp.float32)
    d_mlp_in = jnp.dot(pre_b16, w_up.T, preferred_element_type=jnp.float32)
    g_gain_b = lax.optimization_barrier(jnp.sum(d_mlp_in * normed_b, axis=0))
    g_bias_b = lax.optimization_barrier(jnp.sum(d_mlp_in, axis=0))
    d_resid = grad_out + norm_back(d_mlp_in, normed_b, inverse_b, norm_g[1].astype(jnp.float32))
    resid_b16 = d_resid.astype(jnp.bfloat16)
    g_out = jnp.dot(context.T, resid_b16, preferred_element_type=jnp.float32)
    g_out_bias = lax.optimization_barrier(jnp.sum(d_resid, axis=0))
    d_context = jnp.dot(resid_b16, w_out.T, preferred_element_type=jnp.float32).astype(jnp.bfloat16)
    d_query, d_keys, d_values = attend_back(split_heads(d_context), split_heads(context), queries, keys_all, values_all, log_total, positions, positions)
    d_query = d_query.reshape(-1, model_width)
    d_keys = d_keys.reshape(-1, model_width)
    d_values = d_values.reshape(-1, model_width)
    g_qv_bias = jnp.concatenate([lax.optimization_barrier(jnp.sum(d_query, axis=0)), lax.optimization_barrier(jnp.sum(d_values, axis=0))])
    d_proj = jnp.concatenate([d_query, d_keys, d_values], axis=1).astype(jnp.bfloat16)
    g_qkv = jnp.dot(attn_in.T, d_proj, preferred_element_type=jnp.float32)
    d_attn_in = jnp.dot(d_proj, w_qkv.T, preferred_element_type=jnp.float32)
    g_gain_a = lax.optimization_barrier(jnp.sum(d_attn_in * normed_a, axis=0))
    g_bias_a = lax.optimization_barrier(jnp.sum(d_attn_in, axis=0))
    grad_in = d_resid + norm_back(d_attn_in, normed_a, inverse_a, norm_g[0].astype(jnp.float32))
    layer_grads = (jnp.stack([g_gain_a, g_gain_b]), jnp.stack([g_bias_a, g_bias_b]), g_qkv, g_qv_bias, g_out, g_out_bias, g_up, g_up_bias, g_down, g_down_bias)
    return (grad_in, layer_grads)

def reference(inputs, cotangent, norm_gain, norm_bias, w_qkv, bias_qv, w_out, bias_out, w_up, bias_up, w_down, bias_down):
    params = (norm_gain, norm_bias, w_qkv, bias_qv, w_out, bias_out, w_up, bias_up, w_down, bias_down)
    positions = jnp.arange(SEQ_LEN, dtype=jnp.int32)

    def one_sequence(totals, seq_pair):
        tokens_in, cot_in = seq_pair
        activation = tokens_in.astype(jnp.float32)
        kept_acts = []
        for layer_idx in range(LAYERS):
            layer_params = tuple((member[layer_idx] for member in params))
            activation, saved_acts = forward_layer(activation, layer_params, positions)
            kept_acts.append(saved_acts)
        grad_now = cot_in.astype(jnp.float32)
        per_layer = [None] * LAYERS
        for layer_idx in reversed(range(LAYERS)):
            layer_params = tuple((member[layer_idx] for member in params))
            grad_now, layer_grads = backward_layer(grad_now, layer_params, kept_acts[layer_idx], positions)
            per_layer[layer_idx] = layer_grads
        stacked = tuple((jnp.stack([per_layer[idx_layer][member_idx] for idx_layer in range(LAYERS)]) for member_idx in range(10)))
        new_totals = tuple((total_a + total_b for total_a, total_b in zip(totals, stacked)))
        return (new_totals, (activation.astype(jnp.bfloat16), grad_now))
    init_totals = tuple((jnp.zeros(member.shape, jnp.float32) for member in params))
    totals, (outputs, input_grad) = lax.scan(one_sequence, init_totals, (inputs, cotangent))
    return (outputs, input_grad, totals[0], totals[1], totals[2], totals[3], totals[4], totals[5], totals[6], totals[7], totals[8], totals[9])
```

```python
import functools

import jax
import jax.numpy as jnp
from jax import lax
from jax.experimental import pallas as pl
from jax.experimental.pallas import tpu as pltpu
from jax.sharding import PartitionSpec as P

HEADS = 16
HEAD_DIM = 64

EPS = 1e-05
NEG = -1e30
GELU_C = 0.7978845608028654
GELU_A = 0.044715
F32 = jnp.float32
B16 = jnp.bfloat16
MESH = pl.DeviceIdType.MESH


def norm_apply(values_in, gain_row, bias_row):
    row_mean = jnp.mean(values_in, axis=-1, keepdims=True)
    centered = values_in - row_mean
    variance = jnp.mean(centered * centered, axis=-1, keepdims=True)
    inverse = lax.rsqrt(variance + EPS)
    normed = centered * inverse
    return (normed * gain_row + bias_row, normed, inverse)


def norm_back(grad_in, normed, inverse, gain_row):
    scaled = grad_in * gain_row
    return inverse * (
        scaled
        - jnp.mean(scaled, axis=-1, keepdims=True)
        - normed * jnp.mean(scaled * normed, axis=-1, keepdims=True)
    )


def gelu_parts(pre_act):
    tanh_val = jnp.tanh(GELU_C * (pre_act + GELU_A * pre_act * pre_act * pre_act))
    gelu_value = 0.5 * pre_act * (1.0 + tanh_val)
    gelu_slope = 0.5 * (1.0 + tanh_val) + 0.5 * pre_act * (1.0 - tanh_val * tanh_val) * GELU_C * (
        1.0 + 3.0 * GELU_A * pre_act * pre_act
    )
    return (gelu_value, gelu_slope)


def dot(a, b):
    return jnp.dot(a, b, preferred_element_type=F32)


def dot_nt(a, b):
    return lax.dot_general(a, b, (((1,), (1,)), ((), ())), preferred_element_type=F32)


def dot_tn(a, b):
    return lax.dot_general(a, b, (((0,), (0,)), ((), ())), preferred_element_type=F32)


def greet(peers):
    barrier = pltpu.get_barrier_semaphore()
    for peer in peers:
        pl.semaphore_signal(barrier, inc=1, device_id={"group": peer}, device_id_type=MESH)
    pl.semaphore_wait(barrier, len(peers))


def gather_kernel(groups, x_ref, o_ref, send_sems, recv_sems):
    me = lax.axis_index("group")
    rows = x_ref.shape[0]
    peers = [lax.rem(me + step, groups) for step in range(1, groups)]
    greet(peers)
    here = pl.ds(pl.multiple_of(me * rows, rows), rows)
    copies = []
    for step, peer in enumerate(peers):
        copy = pltpu.make_async_remote_copy(
            src_ref=x_ref,
            dst_ref=o_ref.at[here],
            send_sem=send_sems.at[step],
            recv_sem=recv_sems.at[step],
            device_id={"group": peer},
            device_id_type=MESH,
        )
        copy.start()
        copies.append(copy)
    o_ref[here, :] = x_ref[...]
    for copy in copies:
        copy.wait()


def scatter_kernel(groups, x_ref, o_ref, landed, send_sems, recv_sems):
    me = lax.axis_index("group")
    rows = o_ref.shape[0]
    peers = [lax.rem(me + step, groups) for step in range(1, groups)]
    greet(peers)
    copies = []
    for step, peer in enumerate(peers):
        copy = pltpu.make_async_remote_copy(
            src_ref=x_ref.at[pl.ds(pl.multiple_of(peer * rows, rows), rows)],
            dst_ref=landed.at[step],
            send_sem=send_sems.at[step],
            recv_sem=recv_sems.at[step],
            device_id={"group": peer},
            device_id_type=MESH,
        )
        copy.start()
        copies.append(copy)
    total = x_ref[pl.ds(pl.multiple_of(me * rows, rows), rows), :].astype(F32)
    for step, copy in enumerate(copies):
        copy.wait_recv()
        total = total + landed[step].astype(F32)
    o_ref[...] = total
    for copy in copies:
        copy.wait_send()


VMEM_SPEC = pl.BlockSpec(memory_space=pltpu.VMEM)


def gather_rows(block):
    groups = lax.axis_size("group")
    rows, cols = block.shape
    return pl.pallas_call(
        functools.partial(gather_kernel, groups),
        out_shape=jax.ShapeDtypeStruct((groups * rows, cols), block.dtype),
        in_specs=[VMEM_SPEC],
        out_specs=VMEM_SPEC,
        scratch_shapes=[
            pltpu.SemaphoreType.DMA((groups - 1,)),
            pltpu.SemaphoreType.DMA((groups - 1,)),
        ],
        compiler_params=pltpu.CompilerParams(
            collective_id=0, has_side_effects=True, vmem_limit_bytes=16 * 1024 * 1024
        ),
        cost_estimate=pl.CostEstimate(
            flops=0, bytes_accessed=64 * block.size, transcendentals=0
        ),
    )(block)


def scatter_rows(block):
    groups = lax.axis_size("group")
    rows, cols = block.shape[0] // groups, block.shape[1]
    return pl.pallas_call(
        functools.partial(scatter_kernel, groups),
        out_shape=jax.ShapeDtypeStruct((rows, cols), F32),
        in_specs=[VMEM_SPEC],
        out_specs=VMEM_SPEC,
        scratch_shapes=[
            pltpu.VMEM((groups - 1, rows, cols), block.dtype),
            pltpu.SemaphoreType.DMA((groups - 1,)),
            pltpu.SemaphoreType.DMA((groups - 1,)),
        ],
        compiler_params=pltpu.CompilerParams(
            collective_id=1, has_side_effects=True, vmem_limit_bytes=16 * 1024 * 1024
        ),
        cost_estimate=pl.CostEstimate(
            flops=0, bytes_accessed=64 * block.size // groups, transcendentals=0
        ),
    )(block)


def attention(q, k, v, first_head, heads_here):
    tokens = q.shape[0]
    split = lambda m: m.reshape(tokens, heads_here, HEAD_DIM).transpose(1, 0, 2)
    q, k, v = split(q), split(k), split(v)
    head_ids = (first_head + jnp.arange(heads_here, dtype=jnp.int32)).astype(F32)
    slopes = 2.0 ** (-8.0 * (head_ids + 1.0) / HEADS)
    pos = jnp.arange(tokens, dtype=jnp.int32)
    offset = (pos[:, None] - pos[None, :]).astype(F32)
    raw = jnp.einsum("hqd,hkd->hqk", q, k, preferred_element_type=F32)
    scores = raw * HEAD_DIM ** (-0.5) - slopes[:, None, None] * offset[None]
    scores = jnp.where((offset >= 0.0)[None], scores, NEG)
    row_top = jnp.max(scores, axis=-1, keepdims=True)
    exps_raw = jnp.exp(scores - row_top)
    row_total = jnp.sum(exps_raw, axis=-1, keepdims=True)
    probs = (exps_raw * (1.0 / row_total)).astype(B16)
    context = jnp.einsum("hqk,hkd->hqd", probs, v, preferred_element_type=F32).astype(B16)
    return context.transpose(1, 0, 2).reshape(tokens, -1), (q, k, v, probs, context)


def attention_back(d_context, saved):
    q, k, v, probs, context = saved
    heads_here, tokens, _ = q.shape
    dc = d_context.reshape(tokens, heads_here, HEAD_DIM).transpose(1, 0, 2)
    d_probs = jnp.einsum("hqd,hkd->hqk", dc, v, preferred_element_type=F32)
    delta = jnp.sum(dc.astype(F32) * context.astype(F32), axis=-1, keepdims=True)
    ds = (probs.astype(F32) * (d_probs - delta)).astype(B16)
    scale = HEAD_DIM ** (-0.5)
    dq = jnp.einsum("hqk,hkd->hqd", ds, k, preferred_element_type=F32) * scale
    dk = jnp.einsum("hqk,hqd->hkd", ds, q, preferred_element_type=F32) * scale
    dv = jnp.einsum("hqk,hqd->hkd", probs, dc, preferred_element_type=F32)
    sums = (jnp.sum(dq, axis=1).reshape(-1), jnp.sum(dv, axis=1).reshape(-1))
    join = lambda m: m.astype(B16).transpose(1, 0, 2).reshape(tokens, -1)
    return jnp.concatenate([join(dq), join(dk), join(dv)], axis=1), sums


def local(
    inputs,
    cotangent,
    norm_gain,
    norm_bias,
    w_qkv,
    bias_qv,
    w_out,
    bias_out,
    w_up,
    bias_up,
    w_down,
    bias_down,
):
    groups = lax.axis_size("group")
    replicas = lax.axis_size("replica")
    me = lax.axis_index("group")
    copy_idx = lax.axis_index("replica")
    layers, own, _ = w_qkv.shape
    width = own * groups
    ff_own = w_down.shape[1]
    heads_here = HEADS // groups
    piece = own // replicas

    qkv_piece = lax.dynamic_slice_in_dim(w_qkv, copy_idx * piece, piece, axis=1)
    qkv_piece = qkv_piece.reshape(layers, piece, 3, groups, own).transpose(0, 3, 1, 2, 4)
    qkv_piece = qkv_piece.reshape(layers, groups, piece, 3 * own)
    up_piece = lax.dynamic_slice_in_dim(w_up, copy_idx * piece, piece, axis=1)
    up_piece = up_piece.reshape(layers, piece, groups, ff_own).transpose(0, 2, 1, 3)

    def exchange(block):
        return lax.all_to_all(block, "group", split_axis=0, concat_axis=0, tiled=True)

    def share(block):
        full = lax.all_gather(block, "replica", axis=1, tiled=True)
        return full.reshape(width, -1)

    first = share(exchange(qkv_piece[0]))
    rest = exchange(
        jnp.concatenate([up_piece[l] for l in range(layers)] + [qkv_piece[l] for l in range(1, layers)], axis=2)
    )
    cuts = [ff_own * l for l in range(1, layers + 1)]
    cuts += [ff_own * layers + 3 * own * l for l in range(1, layers - 1)]
    parts = jnp.split(rest, cuts, axis=2)
    wu_cols = [None] * layers
    wq_cols = [first] + [None] * (layers - 1)
    for l in range(layers):
        if l:
            wq_cols[l] = share(parts[layers + l - 1])
        wu_cols[l] = share(parts[l])

    small = jnp.concatenate(
        [norm_gain, norm_bias, bias_qv.reshape(layers, 2, own), bias_out[:, None], bias_down[:, None]],
        axis=1,
    )
    small = lax.all_gather(small, "group", axis=0).astype(F32)
    rows_of = lambda i: small[:, :, i].transpose(1, 0, 2).reshape(layers, width)
    gains = [rows_of(0), rows_of(1)]
    shifts = [rows_of(2), rows_of(3)]
    qv_full = small[:, :, 4:6].transpose(1, 0, 2, 3).reshape(layers, 2 * width)
    q_bias = lax.dynamic_slice_in_dim(qv_full, me * own, own, axis=1)
    v_bias = lax.dynamic_slice_in_dim(qv_full, width + me * own, own, axis=1)
    out_bias, down_bias = rows_of(6), rows_of(7)
    up_bias = bias_up.astype(F32)

    cot_all = gather_rows(cotangent[0])
    x = inputs[0].astype(F32)
    kept = []
    for l in range(layers):
        a1, n0, i0 = norm_apply(x, gains[0][l], shifts[0][l])
        a1_all = gather_rows(a1.astype(B16))
        proj = dot(a1_all, wq_cols[l])
        q = (proj[:, :own] + q_bias[l]).astype(B16)
        k = proj[:, own : 2 * own].astype(B16)
        v = (proj[:, 2 * own :] + v_bias[l]).astype(B16)
        context, attn_saved = attention(q, k, v, me * heads_here, heads_here)
        h = x + scatter_rows(dot(context, w_out[l]).astype(B16)) + out_bias[l]
        a2, n1, i1 = norm_apply(h, gains[1][l], shifts[1][l])
        a2_all = gather_rows(a2.astype(B16))
        value, slope = gelu_parts(dot(a2_all, wu_cols[l]) + up_bias[l])
        hidden = value.astype(B16)
        x = h + scatter_rows(dot(hidden, w_down[l]).astype(B16)) + down_bias[l]
        kept.append((n0, i0, a1_all, attn_saved, context, n1, i1, a2_all, slope, hidden))
    outputs = x.astype(B16)[None]

    def sum_rows(block):
        return lax.all_gather(
            lax.psum_scatter(block, "replica", scatter_dimension=0, tiled=True),
            "replica", axis=0, tiled=True,
        ).astype(F32)

    def sum_cols(block, minor):
        cols = block.shape[1]
        mine = lax.psum_scatter(
            block.reshape(groups, own, cols), "replica", scatter_dimension=1, tiled=True
        )
        mine = exchange(mine).reshape(groups, piece, minor, cols // minor)
        mine = mine.transpose(1, 2, 0, 3).reshape(piece, groups * cols)
        return lax.all_gather(mine, "replica", axis=0, tiled=True).astype(F32)

    g = cotangent[0].astype(F32)
    grads = [None] * layers
    smalls = [None] * layers
    zeros_qv = jnp.zeros((2 * width,), F32)
    for l in reversed(range(layers)):
        n0, i0, a1_all, attn_saved, context, n1, i1, a2_all, slope, hidden = kept[l]
        g_all = cot_all if l == layers - 1 else gather_rows(g.astype(B16))
        gr_down_bias = jnp.sum(g, axis=0)
        d_pre = dot_nt(g_all, w_down[l]) * slope
        gr_up_bias = jnp.sum(d_pre, axis=0)
        pre_b16 = d_pre.astype(B16)
        da2 = scatter_rows(dot_nt(pre_b16, wu_cols[l]).astype(B16))
        gr_down = dot_tn(hidden, g_all).astype(B16)
        gr_up = dot_tn(a2_all, pre_b16).astype(B16)
        gr_gain1, gr_bias1 = jnp.sum(da2 * n1, axis=0), jnp.sum(da2, axis=0)
        dh = g + norm_back(da2, n1, i1, gains[1][l])
        gr_out_bias = jnp.sum(dh, axis=0)
        dh_all = gather_rows(dh.astype(B16))
        dc = dot_nt(dh_all, w_out[l]).astype(B16)
        d_proj, (dq_sum, dv_sum) = attention_back(dc, attn_saved)
        da1 = scatter_rows(dot_nt(d_proj, wq_cols[l]).astype(B16))
        gr_out = dot_tn(context, dh_all).astype(B16)
        gr_qkv = dot_tn(a1_all, d_proj).astype(B16)
        gr_gain0, gr_bias0 = jnp.sum(da1 * n0, axis=0), jnp.sum(da1, axis=0)
        g = dh + norm_back(da1, n0, i0, gains[0][l])
        qv = lax.dynamic_update_slice_in_dim(zeros_qv, dq_sum, me * own, axis=0)
        qv = lax.dynamic_update_slice_in_dim(qv, dv_sum, width + me * own, axis=0)
        smalls[l] = (
            jnp.concatenate([gr_gain0, gr_gain1, gr_bias0, gr_bias1, qv, gr_out_bias, gr_down_bias]),
            gr_up_bias,
        )
        grads[l] = (sum_cols(gr_qkv, 3), sum_rows(gr_out), sum_cols(gr_up, 1), sum_rows(gr_down))

    wide = jnp.stack([s[0] for s in smalls]).reshape(layers, -1, groups, own)
    ups = jnp.stack([s[1] for s in smalls])
    slots = jnp.zeros((layers, groups, ff_own), F32)
    slots = lax.dynamic_update_slice_in_dim(slots, ups[:, None], me, axis=1)
    flat = jnp.concatenate([wide.reshape(layers, -1), slots.reshape(layers, -1)], axis=1)
    total = lax.psum(flat, ("group", "replica"))
    split_at = 8 * width
    wide, slots = total[:, :split_at], total[:, split_at:].reshape(layers, groups, ff_own)
    up_total = lax.dynamic_index_in_dim(slots, me, axis=1, keepdims=False)
    wide = wide.reshape(layers, 8, width)
    own_cols = lax.dynamic_slice_in_dim(wide, me * own, own, axis=2)
    qv_total = lax.dynamic_slice_in_dim(
        wide[:, 4:6].reshape(layers, 2 * width), me * 2 * own, 2 * own, axis=1
    )
    stack = lambda i: jnp.stack([grads[l][i] for l in range(layers)])
    return (
        outputs,
        g[None],
        own_cols[:, 0:2],
        own_cols[:, 2:4],
        stack(0),
        qv_total,
        stack(1),
        own_cols[:, 6],
        stack(2),
        up_total,
        stack(3),
        own_cols[:, 7],
    )


def solution(mesh):
    rows = P("replica", "group", None)
    vec = P(None, None, "group")
    mat = P(None, "group", None)
    bias = P(None, "group")
    params = (vec, vec, mat, bias, mat, bias, mat, bias, mat, bias)
    return jax.shard_map(
        local,
        mesh=mesh,
        in_specs=(rows, rows) + params,
        out_specs=(rows, rows) + params,
        check_vma=False,
    )
```

```python
import functools

import jax
import jax.numpy as jnp
from jax import lax
from jax.experimental import pallas as pl
from jax.experimental.pallas import tpu as pltpu
from jax.sharding import PartitionSpec as P

HEADS = 16
HEAD_DIM = 64

EPS = 1e-05
NEG = -1e30
GELU_C = 0.7978845608028654
GELU_A = 0.044715
F32 = jnp.float32
B16 = jnp.bfloat16
MESH = pl.DeviceIdType.MESH


def norm_apply(values_in, gain_row, bias_row):
    row_mean = jnp.mean(values_in, axis=-1, keepdims=True)
    centered = values_in - row_mean
    variance = jnp.mean(centered * centered, axis=-1, keepdims=True)
    inverse = lax.rsqrt(variance + EPS)
    normed = centered * inverse
    return (normed * gain_row + bias_row, normed, inverse)


def norm_back(grad_in, normed, inverse, gain_row):
    scaled = grad_in * gain_row
    return inverse * (
        scaled
        - jnp.mean(scaled, axis=-1, keepdims=True)
        - normed * jnp.mean(scaled * normed, axis=-1, keepdims=True)
    )


def gelu_parts(pre_act):
    tanh_val = jnp.tanh(GELU_C * (pre_act + GELU_A * pre_act * pre_act * pre_act))
    gelu_value = 0.5 * pre_act * (1.0 + tanh_val)
    gelu_slope = 0.5 * (1.0 + tanh_val) + 0.5 * pre_act * (1.0 - tanh_val * tanh_val) * GELU_C * (
        1.0 + 3.0 * GELU_A * pre_act * pre_act
    )
    return (gelu_value, gelu_slope)


def dot(a, b):
    return jnp.dot(a, b, preferred_element_type=F32)


def dot_nt(a, b):
    return lax.dot_general(a, b, (((1,), (1,)), ((), ())), preferred_element_type=F32)


def dot_tn(a, b):
    return lax.dot_general(a, b, (((0,), (0,)), ((), ())), preferred_element_type=F32)


def greet(peers):
    barrier = pltpu.get_barrier_semaphore()
    for peer in peers:
        pl.semaphore_signal(barrier, inc=1, device_id={"group": peer}, device_id_type=MESH)
    pl.semaphore_wait(barrier, len(peers))


def gather_kernel(groups, x_ref, *refs):
    o_ref, send_sems, recv_sems = refs[-3:]
    me = lax.axis_index("group")
    rows = x_ref.shape[0]
    peers = [lax.rem(me + step, groups) for step in range(1, groups)]
    greet(peers)
    here = pl.ds(pl.multiple_of(me * rows, rows), rows)
    copies = []
    for step, peer in enumerate(peers):
        copy = pltpu.make_async_remote_copy(
            src_ref=x_ref,
            dst_ref=o_ref.at[here],
            send_sem=send_sems.at[step],
            recv_sem=recv_sems.at[step],
            device_id={"group": peer},
            device_id_type=MESH,
        )
        copy.start()
        copies.append(copy)
    o_ref[here, :] = x_ref[...]
    for copy in copies:
        copy.wait()


def scatter_kernel(groups, x_ref, *refs):
    o_ref, landed, send_sems, recv_sems = refs[-4:]
    me = lax.axis_index("group")
    rows = o_ref.shape[0]
    peers = [lax.rem(me + step, groups) for step in range(1, groups)]
    greet(peers)
    copies = []
    for step, peer in enumerate(peers):
        copy = pltpu.make_async_remote_copy(
            src_ref=x_ref.at[pl.ds(pl.multiple_of(peer * rows, rows), rows)],
            dst_ref=landed.at[step],
            send_sem=send_sems.at[step],
            recv_sem=recv_sems.at[step],
            device_id={"group": peer},
            device_id_type=MESH,
        )
        copy.start()
        copies.append(copy)
    total = x_ref[pl.ds(pl.multiple_of(me * rows, rows), rows), :].astype(F32)
    for step, copy in enumerate(copies):
        copy.wait_recv()
        total = total + landed[step].astype(F32)
    o_ref[...] = total
    for copy in copies:
        copy.wait_send()


VMEM_SPEC = pl.BlockSpec(memory_space=pltpu.VMEM)


def gather_rows(block, collective_id=0, after=()):
    groups = lax.axis_size("group")
    rows, cols = block.shape
    return pl.pallas_call(
        functools.partial(gather_kernel, groups),
        out_shape=jax.ShapeDtypeStruct((groups * rows, cols), block.dtype),
        in_specs=[VMEM_SPEC] + [pl.BlockSpec(memory_space=pl.ANY)] * len(after),
        out_specs=VMEM_SPEC,
        scratch_shapes=[
            pltpu.SemaphoreType.DMA((groups - 1,)),
            pltpu.SemaphoreType.DMA((groups - 1,)),
        ],
        compiler_params=pltpu.CompilerParams(
            collective_id=collective_id, has_side_effects=True, vmem_limit_bytes=16 * 1024 * 1024
        ),
        cost_estimate=pl.CostEstimate(
            flops=0, bytes_accessed=640 * block.size, transcendentals=0
        ),
    )(block, *after)


def scatter_rows(block, collective_id=1, after=()):
    groups = lax.axis_size("group")
    rows, cols = block.shape[0] // groups, block.shape[1]
    return pl.pallas_call(
        functools.partial(scatter_kernel, groups),
        out_shape=jax.ShapeDtypeStruct((rows, cols), F32),
        in_specs=[VMEM_SPEC] + [pl.BlockSpec(memory_space=pl.ANY)] * len(after),
        out_specs=VMEM_SPEC,
        scratch_shapes=[
            pltpu.VMEM((groups - 1, rows, cols), block.dtype),
            pltpu.SemaphoreType.DMA((groups - 1,)),
            pltpu.SemaphoreType.DMA((groups - 1,)),
        ],
        compiler_params=pltpu.CompilerParams(
            collective_id=collective_id, has_side_effects=True, vmem_limit_bytes=16 * 1024 * 1024
        ),
        cost_estimate=pl.CostEstimate(
            flops=0, bytes_accessed=640 * block.size // groups, transcendentals=0
        ),
    )(block, *after)


def attention(q, k, v, first_head, heads_here):
    tokens = q.shape[0]
    split = lambda m: m.reshape(tokens, heads_here, HEAD_DIM).transpose(1, 0, 2)
    q, k, v = split(q), split(k), split(v)
    head_ids = (first_head + jnp.arange(heads_here, dtype=jnp.int32)).astype(F32)
    slopes = 2.0 ** (-8.0 * (head_ids + 1.0) / HEADS)
    pos = jnp.arange(tokens, dtype=jnp.int32)
    offset = (pos[:, None] - pos[None, :]).astype(F32)
    raw = jnp.einsum("hqd,hkd->hqk", q, k, preferred_element_type=F32)
    scores = raw * HEAD_DIM ** (-0.5) - slopes[:, None, None] * offset[None]
    scores = jnp.where((offset >= 0.0)[None], scores, NEG)
    row_top = jnp.max(scores, axis=-1, keepdims=True)
    exps_raw = jnp.exp(scores - row_top)
    row_total = jnp.sum(exps_raw, axis=-1, keepdims=True)
    probs = (exps_raw * (1.0 / row_total)).astype(B16)
    context = jnp.einsum("hqk,hkd->hqd", probs, v, preferred_element_type=F32).astype(B16)
    return context.transpose(1, 0, 2).reshape(tokens, -1), (q, k, v, probs, context)


def attention_back(d_context, saved):
    q, k, v, probs, context = saved
    heads_here, tokens, _ = q.shape
    dc = d_context.reshape(tokens, heads_here, HEAD_DIM).transpose(1, 0, 2)
    d_probs = jnp.einsum("hqd,hkd->hqk", dc, v, preferred_element_type=F32)
    delta = jnp.sum(dc.astype(F32) * context.astype(F32), axis=-1, keepdims=True)
    ds = (probs.astype(F32) * (d_probs - delta)).astype(B16)
    scale = HEAD_DIM ** (-0.5)
    dq = jnp.einsum("hqk,hkd->hqd", ds, k, preferred_element_type=F32) * scale
    dk = jnp.einsum("hqk,hqd->hkd", ds, q, preferred_element_type=F32) * scale
    dv = jnp.einsum("hqk,hqd->hkd", probs, dc, preferred_element_type=F32)
    sums = (jnp.sum(dq, axis=1).reshape(-1), jnp.sum(dv, axis=1).reshape(-1))
    join = lambda m: m.astype(B16).transpose(1, 0, 2).reshape(tokens, -1)
    return jnp.concatenate([join(dq), join(dk), join(dv)], axis=1), sums


def local(
    inputs,
    cotangent,
    norm_gain,
    norm_bias,
    w_qkv,
    bias_qv,
    w_out,
    bias_out,
    w_up,
    bias_up,
    w_down,
    bias_down,
):
    groups = lax.axis_size("group")
    replicas = lax.axis_size("replica")
    me = lax.axis_index("group")
    copy_idx = lax.axis_index("replica")
    layers, own, _ = w_qkv.shape
    width = own * groups
    ff_own = w_down.shape[1]
    heads_here = HEADS // groups
    piece = own // replicas

    qkv_piece = lax.dynamic_slice_in_dim(w_qkv, copy_idx * piece, piece, axis=1)
    qkv_piece = qkv_piece.reshape(layers, piece, 3, groups, own).transpose(0, 3, 1, 2, 4)
    qkv_piece = qkv_piece.reshape(layers, groups, piece, 3 * own)
    up_piece = lax.dynamic_slice_in_dim(w_up, copy_idx * piece, piece, axis=1)
    up_piece = up_piece.reshape(layers, piece, groups, ff_own).transpose(0, 2, 1, 3)

    def exchange(block):
        return lax.all_to_all(block, "group", split_axis=0, concat_axis=0, tiled=True)

    def share(block):
        full = lax.all_gather(block, "replica", axis=1, tiled=True)
        return full.reshape(width, -1)

    first = share(exchange(qkv_piece[0]))
    rest = exchange(
        jnp.concatenate([up_piece[l] for l in range(layers)] + [qkv_piece[l] for l in range(1, layers)], axis=2)
    )
    cuts = [ff_own * l for l in range(1, layers + 1)]
    cuts += [ff_own * layers + 3 * own * l for l in range(1, layers - 1)]
    parts = jnp.split(rest, cuts, axis=2)
    wu_cols = [None] * layers
    wq_cols = [first] + [None] * (layers - 1)
    for l in range(layers):
        if l:
            wq_cols[l] = share(parts[layers + l - 1])
        wu_cols[l] = share(parts[l])

    small = jnp.concatenate(
        [norm_gain, norm_bias, bias_qv.reshape(layers, 2, own), bias_out[:, None], bias_down[:, None]],
        axis=1,
    )
    small = lax.all_gather(small, "group", axis=0).astype(F32)
    rows_of = lambda i: small[:, :, i].transpose(1, 0, 2).reshape(layers, width)
    gains = [rows_of(0), rows_of(1)]
    shifts = [rows_of(2), rows_of(3)]
    qv_full = small[:, :, 4:6].transpose(1, 0, 2, 3).reshape(layers, 2 * width)
    q_bias = lax.dynamic_slice_in_dim(qv_full, me * own, own, axis=1)
    v_bias = lax.dynamic_slice_in_dim(qv_full, width + me * own, own, axis=1)
    out_bias, down_bias = rows_of(6), rows_of(7)
    up_bias = bias_up.astype(F32)

    cot_all = gather_rows(cotangent[0])
    x = inputs[0].astype(F32)
    kept = []
    for l in range(layers):
        a1, n0, i0 = norm_apply(x, gains[0][l], shifts[0][l])
        a1_all = gather_rows(a1.astype(B16))
        proj = dot(a1_all, wq_cols[l])
        q = (proj[:, :own] + q_bias[l]).astype(B16)
        k = proj[:, own : 2 * own].astype(B16)
        v = (proj[:, 2 * own :] + v_bias[l]).astype(B16)
        context, attn_saved = attention(q, k, v, me * heads_here, heads_here)
        h = x + scatter_rows(dot(context, w_out[l]).astype(B16)) + out_bias[l]
        a2, n1, i1 = norm_apply(h, gains[1][l], shifts[1][l])
        a2_all = gather_rows(a2.astype(B16))
        value, slope = gelu_parts(dot(a2_all, wu_cols[l]) + up_bias[l])
        hidden = value.astype(B16)
        x = h + scatter_rows(dot(hidden, w_down[l]).astype(B16)) + down_bias[l]
        kept.append((n0, i0, a1_all, attn_saved, context, n1, i1, a2_all, slope, hidden))
    outputs = x.astype(B16)[None]

    def reduce_pair(cols_grad, rows_grad):
        cols = cols_grad.shape[1]
        blocks = [cols_grad[i * own : (i + 1) * own] for i in range(groups)]
        folds = rows_grad.shape[0] // own
        blocks += [rows_grad[i * own : (i + 1) * own] for i in range(folds)]
        return lax.psum_scatter(
            jnp.concatenate(blocks, axis=1), "replica", scatter_dimension=0, tiled=True
        )

    def share_pair(mine, cols, minor):
        cut = groups * cols
        left = exchange(mine[:, :cut].reshape(piece, groups, cols).transpose(1, 0, 2))
        left = left.reshape(groups, piece, minor, cols // minor).transpose(1, 2, 0, 3)
        mine = jnp.concatenate([left.reshape(piece, cut), mine[:, cut:]], axis=1)
        return lax.all_gather(mine, "replica", axis=0, tiled=True)

    def unpack_pair(full, cols):
        cut = groups * cols
        folds = (full.shape[1] - cut) // width
        rows = [full[:, cut + i * width : cut + (i + 1) * width] for i in range(folds)]
        return full[:, :cut].astype(F32), jnp.concatenate(rows, axis=0).astype(F32)

    g = cotangent[0].astype(F32)
    grads = [None] * layers
    smalls = [None] * layers
    held = {}
    zeros_qv = jnp.zeros((2 * width,), F32)
    for l in reversed(range(layers)):
        n0, i0, a1_all, attn_saved, context, n1, i1, a2_all, slope, hidden = kept[l]
        prev = held.get(l + 1)
        if prev is None:
            g_all = cot_all
        else:
            g_all = gather_rows(g.astype(B16), 3, (prev["ffn_sum"],))
            prev["ffn"] = share_pair(prev["ffn_sum"], ff_own, 1)
        gr_down_bias = jnp.sum(g, axis=0)
        d_pre = dot_nt(g_all, w_down[l]) * slope
        gr_up_bias = jnp.sum(d_pre, axis=0)
        pre_b16 = d_pre.astype(B16)
        da2 = scatter_rows(dot_nt(pre_b16, wu_cols[l]).astype(B16))
        gr_down = dot_tn(hidden, g_all).astype(B16)
        gr_up = dot_tn(a2_all, pre_b16).astype(B16)
        held[l] = {"ffn_sum": reduce_pair(gr_up, gr_down)}
        gr_gain1, gr_bias1 = jnp.sum(da2 * n1, axis=0), jnp.sum(da2, axis=0)
        dh = g + norm_back(da2, n1, i1, gains[1][l])
        gr_out_bias = jnp.sum(dh, axis=0)
        if prev is None:
            dh_all = gather_rows(dh.astype(B16))
        else:
            dh_all = gather_rows(dh.astype(B16), 4, (prev["attn_sum"], prev["ffn"]))
            prev["attn"] = share_pair(prev["attn_sum"], 3 * own, 3)
        dc = dot_nt(dh_all, w_out[l]).astype(B16)
        d_proj, (dq_sum, dv_sum) = attention_back(dc, attn_saved)
        da1_part = dot_nt(d_proj, wq_cols[l]).astype(B16)
        da1 = scatter_rows(da1_part) if prev is None else scatter_rows(da1_part, 5, (held[l]["ffn_sum"],))
        gr_out = dot_tn(context, dh_all).astype(B16)
        gr_qkv = dot_tn(a1_all, d_proj).astype(B16)
        gr_gain0, gr_bias0 = jnp.sum(da1 * n0, axis=0), jnp.sum(da1, axis=0)
        g = dh + norm_back(da1, n0, i0, gains[0][l])
        qv = lax.dynamic_update_slice_in_dim(zeros_qv, dq_sum, me * own, axis=0)
        qv = lax.dynamic_update_slice_in_dim(qv, dv_sum, width + me * own, axis=0)
        smalls[l] = (
            jnp.concatenate([gr_gain0, gr_gain1, gr_bias0, gr_bias1, qv, gr_out_bias, gr_down_bias]),
            gr_up_bias,
        )
        held[l]["attn_sum"] = reduce_pair(gr_qkv, gr_out)

    for l in range(layers):
        ffn = held[l]["ffn"] if "ffn" in held[l] else share_pair(held[l]["ffn_sum"], ff_own, 1)
        attn = held[l]["attn"] if "attn" in held[l] else share_pair(held[l]["attn_sum"], 3 * own, 3)
        grads[l] = unpack_pair(attn, 3 * own) + unpack_pair(ffn, ff_own)

    wide = jnp.stack([s[0] for s in smalls])
    per_owner = lambda lo, n: wide[:, lo * width : (lo + n) * width].reshape(layers, n, groups, own)
    gain_bias = per_owner(0, 4).transpose(2, 0, 1, 3)
    qv = wide[:, 4 * width : 6 * width].reshape(layers, groups, 2, own).transpose(1, 0, 2, 3)
    dense = per_owner(6, 2).transpose(2, 0, 1, 3)
    wide = jnp.concatenate([gain_bias, qv, dense], axis=2)
    mine = scatter_rows(wide.reshape(groups * layers * 8, own), 2)
    ups = jnp.stack([s[1] for s in smalls])
    flat = jnp.concatenate([mine.reshape(-1), ups.reshape(-1)]).reshape(-1, 128)
    total = lax.psum(flat, "replica").reshape(-1)
    cut = layers * 8 * own
    own_cols = total[:cut].reshape(layers, 8, own)
    up_total = total[cut:].reshape(layers, ff_own)
    qv_total = own_cols[:, 4:6].reshape(layers, 2 * own)
    stack = lambda i: jnp.stack([grads[l][i] for l in range(layers)])
    return (
        outputs,
        g[None],
        own_cols[:, 0:2],
        own_cols[:, 2:4],
        stack(0),
        qv_total,
        stack(1),
        own_cols[:, 6],
        stack(2),
        up_total,
        stack(3),
        own_cols[:, 7],
    )


def solution(mesh):
    rows = P("replica", "group", None)
    vec = P(None, None, "group")
    mat = P(None, "group", None)
    bias = P(None, "group")
    params = (vec, vec, mat, bias, mat, bias, mat, bias, mat, bias)
    return jax.shard_map(
        local,
        mesh=mesh,
        in_specs=(rows, rows) + params,
        out_specs=(rows, rows) + params,
        check_vma=False,
    )
```
